32 devices in a mesh: lat: 4 (over y, x), lon: 8 (over z, core).
Axes of the slice: x: 2, y: 2, z: 4, core: 2. Of those that a mesh axis runs over, the one named last changes fastest.
Arguments:
- prior: float32 [64, 128, 1024], P(None, 'lat', 'lon'), may hold values from 0.1 to 1
- habitat: bfloat16 [32, 128, 1024], P(None, 'lat', 'lon'), may hold values from -6 to 6
- kappa: float32 [128, 1024], P('lat', 'lon'), may hold values from 0.03 to 0.24
- ocean_mask: int32 [128, 1024], P('lat', 'lon'), may hold values 0 or 1
- profiles: float32 [256, 32], P('lon'), may hold values from -6 to 6
- tag_ids: int32 [256], P('lon'), may hold values from 0 to 63
Outputs:
- posterior: float32 [64, 128, 1024], P(None, 'lat', 'lon')
- log_evidence: float32 [64], replicated
The draws below stay inside these ranges and needn't reach their ends.
All inputs are finite; a program needn't handle non-finite values. No bound on the sum of `ocean_mask` on one device may be relied on, other than what follows from the above.
Results may differ from the reference program's by a relative error of at most 0.0003.
Values sent between devices are 32-bit elements; how exact they have to be, the bound alone decides.
A program may use at most 64 MiB of HBM per device.

```python
import math
import jax
import jax.numpy as jnp
from jax import lax

TAGS = 64
LEVELS = 32
PROFILES = 256
NLAT = 128
NLON = 1024


def touch_ends(array, stream_key, smallest, high):
    shape = array.shape
    index_at = [jax.random.randint(jax.random.fold_in(stream_key, axis), (), 0, shape[axis]) for axis in range(len(shape))]
    array = array.at[tuple(index_at)].set(smallest)
    longest = shape.index(max(shape))
    index_at[longest] = (index_at[longest] + 1) % shape[longest]
    return array.at[tuple(index_at)].set(high)


def block_levels(stream_key, extent, cuts, smallest, top_value):
    def one(position, parts):
        heights = jax.random.uniform(jax.random.fold_in(jax.random.fold_in(stream_key, 6), position), (parts,), jnp.float32, smallest / len(cuts), top_value / len(cuts))
        return jnp.repeat(jnp.exp(heights), extent[position] // parts).reshape((-1,) + (1,) * (len(extent) - position - 1))

    level = one(*cuts[0])
    for cut in cuts[1:]:
        level = level * one(*cut)
    return level


def noise(rng, dims, deviation, most, pieces=(), held_as=jnp.bfloat16):
    factor_of = block_levels(rng, dims, pieces, -0.22, 0.18) if pieces else 1.0
    array = jax.random.normal(rng, dims, jnp.float32) * deviation * factor_of
    return jnp.minimum(jnp.maximum(array, -most), most).astype(held_as)


def setup_inputs(seed: int = 0) -> dict:
    key_of = jax.random.split(jax.random.key(seed), 7)
    return {
        "prior": jnp.clip(jnp.exp(math.log(1.0) - 2.3025851 * jax.random.uniform(key_of[0], (TAGS, NLAT, NLON), jnp.float32) ** block_levels(key_of[0], (TAGS, NLAT, NLON), ((1, 4), (2, 8)), -0.2, 0.2)), 0.1, 1.0),
        "habitat": noise(key_of[1], (LEVELS, NLAT, NLON), 1.0, 6.0, ((1, 4), (2, 8))),
        "kappa": jnp.clip(jnp.exp(math.log(0.24) - 2.0794415 * jax.random.uniform(key_of[2], (NLAT, NLON), jnp.float32) ** block_levels(key_of[2], (NLAT, NLON), ((0, 4), (1, 8)), -0.2, 0.2)), 0.03, 0.24),
        "ocean_mask": touch_ends((jax.random.randint(key_of[3], (NLAT, NLON), 0, 4) < 3).astype(jnp.int32), jax.random.fold_in(key_of[3], 1), 0, 1),
        "profiles": noise(key_of[4], (PROFILES, LEVELS), 1.0, 6.0, ((0, 8),), jnp.float32),
        "tag_ids": touch_ends(jax.random.randint(key_of[5], (PROFILES,), 0, TAGS), jax.random.fold_in(key_of[5], 1), 0, TAGS - 1).astype(jnp.int32),
    }


reach_weights = (0.4, 0.3, 0.2, 0.1)
misfit_scale = 8.0


def substep(field, coeff, ocean):
    rows = field.shape[0]
    padded = jnp.pad(field, ((4, 4), (0, 0)))
    accum = -4.0 * field
    for reach in range(1, 5):
        weight = reach_weights[reach - 1]
        accum = accum + weight * (padded[4 + reach:4 + reach + rows] + padded[4 - reach:4 - reach + rows]
                                  + jnp.roll(field, -reach, 1) + jnp.roll(field, reach, 1))
    return (field + coeff * accum) * ocean


def reference(prior, habitat, kappa, ocean_mask, profiles, tag_ids):
    ocean = ocean_mask.astype(jnp.float32)
    onehot = (tag_ids[:, None] == jnp.arange(TAGS, dtype=jnp.int32)[None, :]).astype(jnp.float32)
    first_moment = jnp.dot(onehot.T, profiles, precision=lax.Precision.HIGHEST)
    second_moment = jnp.dot(onehot.T, jnp.sum(profiles * profiles, 1), precision=lax.Precision.HIGHEST)
    count = jnp.sum(onehot, 0)
    habfloat = habitat.astype(jnp.float32)
    habsquare = jnp.sum(habfloat * habfloat, 0)

    def per_tag(items):
        field, first, second, number = items
        field = field * ocean
        field = substep(field, kappa, ocean)
        field = substep(field, kappa, ocean)
        crossed = jnp.tensordot(first, habfloat, axes=1, precision=lax.Precision.HIGHEST)
        misfit = second - 2.0 * crossed + number * habsquare
        return field * jnp.exp(-misfit / (misfit_scale * LEVELS))

    updated = lax.map(per_tag, (prior, first_moment, second_moment, count))
    total = jnp.sum(updated, axis=(1, 2))
    cells = jnp.float32(NLAT * NLON)
    return updated * (cells / total)[:, None, None], jnp.log(total / cells)
```

```python
import functools

import jax
import jax.numpy as jnp
from jax import lax
from jax.experimental import pallas as pl
from jax.experimental.pallas import tpu as pltpu
from jax.sharding import PartitionSpec as P

MESH = pl.DeviceIdType.MESH
HIGHEST = lax.Precision.HIGHEST
misfit_scale = 8.0
DEEP = 8
REACH = 4


def spread(rows):
    count, lanes = rows.shape
    return jnp.broadcast_to(rows[:, None, :], (count, 8, lanes)).reshape(count * 8, lanes)


def kernel(
    dims, prior3, prior2, hab2, kappa, mask, profiles, ids, out2, logev,
    pr, hb, hf, ext, one, lik, ak, aux_lo, aux_hi, bulk_lo, bulk_hi, kb, khb,
    px, px_left, px_right, he, ce, h1, mom, acc, tot1, tot2,
    loc_sem, mom_s, mom_r, px_s, px_r, aux_s, aux_r, bulk_s, bulk_r, cor_s, cor_r,
    t1_s, t1_r, t2_s, t2_r,
):
    n_lat, n_lon, tags, levels, rows, lanes = dims
    groups = tags // 8
    erows = rows + 2 * DEEP
    hrows = rows + 2 * REACH
    half = tags // 2
    lat, lon = lax.axis_index("lat"), lax.axis_index("lon")
    has_lo, has_hi = lat > 0, lat < n_lat - 1
    left, right = lax.rem(lon + n_lon - 1, n_lon), lax.rem(lon + 1, n_lon)

    own_prior = pltpu.make_async_copy(prior2, pr, loc_sem.at[0])
    own_hab = pltpu.make_async_copy(hab2, hb, loc_sem.at[1])
    own_prior.start()
    own_hab.start()

    barrier = pltpu.get_barrier_semaphore()
    for k in range(1, n_lon):
        pl.semaphore_signal(
            barrier, inc=1, device_id={"lon": lax.rem(lon + k, n_lon)}, device_id_type=MESH
        )
    for k in range(1, n_lat):
        pl.semaphore_signal(
            barrier, inc=1, device_id={"lat": lax.rem(lat + k, n_lat)}, device_id_type=MESH
        )

    def remote(src, dst, send, recv, where):
        return pltpu.make_async_remote_copy(
            src_ref=src, dst_ref=dst, send_sem=send, recv_sem=recv, device_id=where,
            device_id_type=MESH,
        )

    lane = lax.broadcasted_iota(jnp.int32, (8, lanes), 1)
    ocean = mask[...].astype(jnp.float32)
    ko = kappa[...] * ocean
    ak[0] = ocean
    ak[1] = ko
    prof = profiles[...]
    local = prof.shape[0]
    squares = jnp.sum(prof * prof, 1, keepdims=True)
    table = jnp.concatenate(
        [
            prof,
            squares,
            jnp.ones((local, 1), jnp.float32),
            jnp.zeros((local, 128 - levels - 2), jnp.float32),
        ],
        axis=1,
    )
    onehot = (
        lax.broadcasted_iota(jnp.int32, (tags, local), 0) == ids[...]
    ).astype(jnp.float32)
    sums = jnp.dot(onehot, table, precision=HIGHEST, preferred_element_type=jnp.float32)
    mom[lon] = sums[:half] + pltpu.roll(sums[half:], 64, 1)
    folded = pltpu.roll(ko, DEEP, 1)
    folded = jnp.where(lax.broadcasted_iota(jnp.int32, (rows, lanes), 1) < 16, folded, 0.0)
    for step in (16, 32, 64):
        folded = folded + pltpu.roll(folded, step, 1)
    px[pl.ds(rows * 8, rows), :] = folded

    pl.semaphore_wait(barrier, n_lon - 1 + n_lat - 1)

    to_hi_aux = remote(
        ak.at[:, rows - DEEP : rows, :], aux_lo, aux_s.at[0], aux_r.at[0], {"lat": lat + 1}
    )
    to_lo_aux = remote(ak.at[:, 0:DEEP, :], aux_hi, aux_s.at[1], aux_r.at[1], {"lat": lat - 1})

    def to_hi(g):
        return remote(
            prior3.at[pl.ds(g * 8, 8), rows - DEEP : rows, :],
            bulk_lo.at[pl.ds(g * 8, 8)],
            bulk_s.at[0, g],
            bulk_r.at[0, g],
            {"lat": lat + 1},
        )

    def to_lo(g):
        return remote(
            prior3.at[pl.ds(g * 8, 8), 0:DEEP, :],
            bulk_hi.at[pl.ds(g * 8, 8)],
            bulk_s.at[1, g],
            bulk_r.at[1, g],
            {"lat": lat - 1},
        )

    moment_copies = []
    for k in range(1, n_lon):
        copy = remote(
            mom.at[lon], mom.at[lon], mom_s.at[k - 1], mom_r.at[k - 1],
            {"lon": lax.rem(lon + k, n_lon)},
        )
        copy.start()
        moment_copies.append(copy)

    early = groups // 2

    @pl.when(has_hi)
    def _():
        to_hi_aux.start()
        for g in range(early):
            to_hi(g).start()

    @pl.when(has_lo)
    def _():
        to_lo_aux.start()
        for g in range(early):
            to_lo(g).start()

    @pl.when(jnp.logical_not(has_lo))
    def _():
        bulk_lo[...] = jnp.zeros_like(bulk_lo)
        aux_lo[...] = jnp.zeros_like(aux_lo)
        he[0 : REACH * 8, :] = jnp.zeros((REACH * 8, lanes), jnp.float32)

    @pl.when(jnp.logical_not(has_hi))
    def _():
        bulk_hi[...] = jnp.zeros_like(bulk_hi)
        aux_hi[...] = jnp.zeros_like(aux_hi)
        he[(REACH + rows) * 8 : hrows * 8, :] = jnp.zeros((REACH * 8, lanes), jnp.float32)

    own_prior.wait()

    def pack(a, carry):
        wet = jnp.broadcast_to(ak[0, pl.ds(a, 1), :], (8, lanes))
        packed = jnp.zeros((8, lanes), jnp.float32)
        for g in range(groups):
            value = pr[pl.ds(g * 8 * rows + a, 8, stride=rows), :] * wet
            ext[pl.ds(pl.multiple_of((g * erows + DEEP + a) * 8, 8), 8), :] = value
            turned = pltpu.roll(value, (DEEP + 16 * g) % lanes, 1)
            packed = jnp.where((lane >= 16 * g) & (lane < 16 * g + 16), turned, packed)
        px[pl.ds(pl.multiple_of(a * 8, 8), 8), :] = packed
        return carry

    lax.fori_loop(0, rows, pack, 0, unroll=2)

    to_right = remote(px, px_left, px_s.at[0], px_r.at[0], {"lon": right})
    to_left = remote(px, px_right, px_s.at[1], px_r.at[1], {"lon": left})
    to_right.start()
    to_left.start()

    own_hab.wait()
    hf[...] = hb[...].astype(jnp.float32)
    for copy in moment_copies:
        copy.wait()
    total_moments = mom[0]
    for k in range(1, n_lon):
        total_moments = total_moments + mom[k]
    moments = jnp.concatenate([total_moments, pltpu.roll(total_moments, 64, 1)], axis=0)
    tag_lane = lax.broadcasted_iota(jnp.int32, (tags, lanes), 1)
    second = jnp.broadcast_to(moments[:, levels : levels + 1], (tags, lanes))
    count = jnp.broadcast_to(moments[:, levels + 1 : levels + 2], (tags, lanes))
    first = jnp.where(tag_lane < levels, moments, 0.0)
    top = first.astype(jnp.bfloat16).astype(jnp.float32)
    rest = first - top
    middle = rest.astype(jnp.bfloat16).astype(jnp.float32)
    bottom = (rest - middle).astype(jnp.bfloat16).astype(jnp.float32)
    split = (top + pltpu.roll(middle, levels, 1) + pltpu.roll(bottom, 2 * levels, 1)).astype(
        jnp.bfloat16
    )
    pad = jnp.zeros((lanes - 3 * levels, lanes), jnp.bfloat16)

    def likelihood(a, carry):
        field = hf[pl.ds(a, levels, stride=rows), :]
        square = jnp.sum(field * field, 0, keepdims=True)
        narrow = field.astype(jnp.bfloat16)
        crossed = jnp.dot(
            split,
            jnp.concatenate([narrow, narrow, narrow, pad], axis=0),
            preferred_element_type=jnp.float32,
        )
        misfit = second - 2.0 * crossed + count * square
        value = jnp.exp(misfit * (-1.0 / (misfit_scale * levels)))
        for g in range(groups):
            lik[pl.ds(pl.multiple_of((g * rows + a) * 8, 8), 8), :] = value[g * 8 : g * 8 + 8]
        return carry

    lax.fori_loop(0, rows, likelihood, 0, unroll=2)

    to_right.wait()
    to_left.wait()
    low_side = lax.rem(lax.broadcasted_iota(jnp.int32, (64, lanes), 1), 16) < 8
    for b in range(rows // 8):
        he[(REACH + 8 * b) * 8 : (REACH + 8 * b + 8) * 8, :] = jnp.where(
            low_side, px_left[b * 64 : b * 64 + 64, :], px_right[b * 64 : b * 64 + 64, :]
        )
    low_rows = lax.rem(lax.broadcasted_iota(jnp.int32, (rows, lanes), 1), 16) < 8
    ko_side = jnp.where(
        low_rows, px_left[rows * 8 : rows * 9, :], px_right[rows * 8 : rows * 9, :]
    )
    khb[...] = spread(ko_side)

    cor_hi = remote(
        he.at[rows * 8 : (rows + REACH) * 8, :], he.at[0 : REACH * 8, :],
        cor_s.at[0], cor_r.at[0], {"lat": lat + 1},
    )
    cor_lo = remote(
        he.at[REACH * 8 : 2 * REACH * 8, :], he.at[(REACH + rows) * 8 : hrows * 8, :],
        cor_s.at[1], cor_r.at[1], {"lat": lat - 1},
    )

    @pl.when(has_hi)
    def _():
        cor_hi.start()
        for g in range(early, groups):
            to_hi(g).start()

    @pl.when(has_lo)
    def _():
        cor_lo.start()
        for g in range(early, groups):
            to_lo(g).start()

    @pl.when(has_lo)
    def _():
        to_hi_aux.wait_recv()
        cor_hi.wait_recv()

    @pl.when(has_hi)
    def _():
        to_lo_aux.wait_recv()
        cor_lo.wait_recv()

    kb[0 : REACH * 8, :] = spread(aux_lo[1])[REACH * 8 :]
    kb[REACH * 8 : (REACH + rows) * 8, :] = spread(ak[1])
    kb[(REACH + rows) * 8 :, :] = spread(aux_hi[1])[: REACH * 8]

    def lon_sum(low, high):
        total = pltpu.roll(low, REACH, 1) + pltpu.roll(high, lanes - REACH, 1)
        for d in range(1, REACH):
            total = total + (5.0 - d) * (pltpu.roll(low, d, 1) + pltpu.roll(high, lanes - d, 1))
        return total

    def lat_sum(ref, at):
        total = ref[pl.ds(at - 8 * REACH, 64), :] + ref[pl.ds(at + 8 * REACH, 64), :]
        for d in range(1, REACH):
            total = total + (5.0 - d) * (
                ref[pl.ds(at - 8 * d, 64), :] + ref[pl.ds(at + 8 * d, 64), :]
            )
        return total

    def across(field):
        from_low = jnp.where(low_side, field, 0.0)
        from_high = jnp.where(low_side, 0.0, field)
        low, high = pltpu.roll(from_low, REACH, 1), pltpu.roll(from_high, lanes - REACH, 1)
        for d in range(1, REACH):
            low = low + (5.0 - d) * pltpu.roll(from_low, d, 1)
            high = high + (5.0 - d) * pltpu.roll(from_high, lanes - d, 1)
        return jnp.where(low_side, high, low)

    for b in range(hrows // 8):
        ce[b * 64 : b * 64 + 64, :] = across(he[b * 64 : b * 64 + 64, :])

    for b in range(rows // 8):
        at = (REACH + 8 * b) * 8
        side = he[at : at + 64, :]
        inner = px[b * 64 : b * 64 + 64, :]
        z_left = jnp.where(low_side, side, inner)
        z_right = jnp.where(low_side, inner, side)
        along = jnp.where(low_side, lon_sum(z_left, z_left), lon_sum(z_right, z_right))
        h1[b * 64 : b * 64 + 64, :] = across(
            side
            + khb[b * 64 : b * 64 + 64, :] * (0.1 * (along + lat_sum(he, at)) - 4.0 * side)
        )

    weights = [
        (
            jnp.concatenate([jnp.where(lane >= d, 5.0 - d, 0.0)] * 8, axis=0),
            jnp.concatenate([jnp.where(lane < lanes - d, 5.0 - d, 0.0)] * 8, axis=0),
        )
        for d in range(1, REACH + 1)
    ]
    at_edge = jnp.concatenate([(lane < REACH) | (lane >= lanes - REACH)] * 8, axis=0)
    low_flat = bulk_lo.reshape(tags * DEEP, lanes)
    high_flat = bulk_hi.reshape(tags * DEEP, lanes)
    acc[...] = jnp.zeros_like(acc)

    def sweep(center, sides, shift, coeff, ref, at):
        along = jnp.where(at_edge, pltpu.roll(sides, shift, 1), 0.0) + lat_sum(ref, at)
        for d in range(1, REACH + 1):
            up, down = weights[d - 1]
            along = along + up * pltpu.roll(center, d, 1) + down * pltpu.roll(center, lanes - d, 1)
        return center + coeff * (0.1 * along - 4.0 * center)

    def group(g, carry):
        @pl.when(has_lo)
        def _():
            to_hi(g).wait_recv()

        @pl.when(has_hi)
        def _():
            to_lo(g).wait_recv()

        base = g * erows * 8
        for a in range(DEEP):
            ext[pl.ds(pl.multiple_of(base + a * 8, 8), 8), :] = low_flat[
                pl.ds(g * 64 + a, 8, stride=DEEP), :
            ] * jnp.broadcast_to(aux_lo[0, a : a + 1, :], (8, lanes))
            ext[pl.ds(pl.multiple_of(base + (DEEP + rows + a) * 8, 8), 8), :] = high_flat[
                pl.ds(g * 64 + a, 8, stride=DEEP), :
            ] * jnp.broadcast_to(aux_hi[0, a : a + 1, :], (8, lanes))
        shift = lax.rem(lanes - DEEP - 16 * g + lanes, lanes)
        for b in range(hrows // 8):
            at = pl.multiple_of(base + (REACH + 8 * b) * 8, 8)
            one[b * 64 : b * 64 + 64, :] = sweep(
                ext[pl.ds(at, 64), :],
                ce[b * 64 : b * 64 + 64, :],
                shift,
                kb[b * 64 : b * 64 + 64, :],
                ext,
                at,
            )
        partial = jnp.zeros((8, lanes), jnp.float32)
        for b in range(rows // 8):
            at = (REACH + 8 * b) * 8
            here = pl.ds(pl.multiple_of(g * rows * 8 + b * 64, 8), 64)
            updated = (
                sweep(
                    one[at : at + 64, :],
                    h1[b * 64 : b * 64 + 64, :],
                    shift,
                    kb[at : at + 64, :],
                    one,
                    at,
                )
                * lik[here, :]
            )
            lik[here, :] = updated
            partial = partial + jnp.sum(updated.reshape(8, 8, lanes), 0)
        acc[pl.ds(pl.multiple_of(g * 8, 8), 8), :] = partial
        return carry

    lax.fori_loop(0, groups, group, 0)

    row = lax.dot_general(
        jnp.ones((8, lanes), jnp.float32), acc[...], (((1,), (1,)), ((), ())),
        precision=HIGHEST, preferred_element_type=jnp.float32,
    )
    tot1[lon] = row[0:1]
    copies = []
    for k in range(1, n_lon):
        copy = remote(
            tot1.at[lon], tot1.at[lon], t1_s.at[k - 1], t1_r.at[k - 1],
            {"lon": lax.rem(lon + k, n_lon)},
        )
        copy.start()
        copies.append(copy)
    for copy in copies:
        copy.wait()
    total = tot1[0]
    for k in range(1, n_lon):
        total = total + tot1[k]
    tot2[lat] = total
    copies = []
    for k in range(1, n_lat):
        copy = remote(
            tot2.at[lat], tot2.at[lat], t2_s.at[k - 1], t2_r.at[k - 1],
            {"lat": lax.rem(lat + k, n_lat)},
        )
        copy.start()
        copies.append(copy)
    for copy in copies:
        copy.wait()
    total = tot2[0]
    for k in range(1, n_lat):
        total = total + tot2[k]
    cells = float(n_lat * n_lon * rows * lanes)
    logev[...] = jnp.log(total[:, :tags] / cells)
    first_row = lax.broadcasted_iota(jnp.int32, (8, lanes), 0) == 0
    column = lax.dot_general(
        jnp.where(first_row, jnp.broadcast_to(total, (8, lanes)), 0.0),
        jnp.ones((8, lanes), jnp.float32),
        (((0,), (0,)), ((), ())),
        precision=HIGHEST, preferred_element_type=jnp.float32,
    )
    acc[...] = cells / column

    def finish(a, carry):
        for g in range(groups):
            out2[pl.ds(g * 8 * rows + a, 8, stride=rows), :] = (
                lik[pl.ds(pl.multiple_of((g * rows + a) * 8, 8), 8), :]
                * acc[g * 8 : g * 8 + 8, :]
            )
        return carry

    lax.fori_loop(0, rows, finish, 0, unroll=2)

    @pl.when(has_hi)
    def _():
        to_hi_aux.wait_send()
        cor_hi.wait_send()
        for g in range(groups):
            to_hi(g).wait_send()

    @pl.when(has_lo)
    def _():
        to_lo_aux.wait_send()
        cor_lo.wait_send()
        for g in range(groups):
            to_lo(g).wait_send()


def body(n_lat, n_lon, prior, habitat, kappa, ocean_mask, profiles, tag_ids):
    tags, rows, lanes = prior.shape
    levels = habitat.shape[0]
    groups = tags // 8
    erows, hrows = rows + 2 * DEEP, rows + 2 * REACH
    f32 = jnp.float32
    flat = (tags * rows, lanes)
    vmem = pl.BlockSpec(memory_space=pltpu.VMEM)
    hbm = pl.BlockSpec(memory_space=pl.ANY)
    dma = pltpu.SemaphoreType.DMA
    posterior, logev = pl.pallas_call(
        functools.partial(kernel, (n_lat, n_lon, tags, levels, rows, lanes)),
        name="filter_step",
        out_shape=(jax.ShapeDtypeStruct(flat, f32), jax.ShapeDtypeStruct((1, tags), f32)),
        in_specs=[hbm, hbm, hbm, vmem, vmem, vmem, vmem],
        out_specs=(vmem, vmem),
        scratch_shapes=[
            pltpu.VMEM(flat, f32),
            pltpu.VMEM((levels * rows, lanes), habitat.dtype),
            pltpu.VMEM((levels * rows, lanes), f32),
            pltpu.VMEM((groups * erows * 8, lanes), f32),
            pltpu.VMEM((hrows * 8, lanes), f32),
            pltpu.VMEM((groups * rows * 8, lanes), f32),
            pltpu.VMEM((2, rows, lanes), f32),
            pltpu.VMEM((2, DEEP, lanes), f32),
            pltpu.VMEM((2, DEEP, lanes), f32),
            pltpu.VMEM((tags, DEEP, lanes), f32),
            pltpu.VMEM((tags, DEEP, lanes), f32),
            pltpu.VMEM((hrows * 8, lanes), f32),
            pltpu.VMEM((rows * 8, lanes), f32),
            pltpu.VMEM((rows * 9, lanes), f32),
            pltpu.VMEM((rows * 9, lanes), f32),
            pltpu.VMEM((rows * 9, lanes), f32),
            pltpu.VMEM((hrows * 8, lanes), f32),
            pltpu.VMEM((hrows * 8, lanes), f32),
            pltpu.VMEM((rows * 8, lanes), f32),
            pltpu.VMEM((n_lon, tags // 2, lanes), f32),
            pltpu.VMEM((lanes, lanes), f32),
            pltpu.VMEM((n_lon, 1, lanes), f32),
            pltpu.VMEM((n_lat, 1, lanes), f32),
            dma((2,)),
            dma((n_lon - 1,)),
            dma((n_lon - 1,)),
            dma((2,)),
            dma((2,)),
            dma((2,)),
            dma((2,)),
            dma((2, groups)),
            dma((2, groups)),
            dma((2,)),
            dma((2,)),
            dma((n_lon - 1,)),
            dma((n_lon - 1,)),
            dma((n_lat - 1,)),
            dma((n_lat - 1,)),
        ],
        compiler_params=pltpu.CompilerParams(collective_id=0, has_side_effects=True),
    )(
        prior,
        prior.reshape(flat),
        habitat.reshape(levels * rows, lanes),
        kappa,
        ocean_mask,
        profiles,
        tag_ids[None, :],
    )
    return posterior.reshape(prior.shape), logev[0]


def solution(mesh):
    placed = (
        P(None, "lat", "lon"),
        P(None, "lat", "lon"),
        P("lat", "lon"),
        P("lat", "lon"),
        P("lon", None),
        P("lon"),
    )
    return jax.shard_map(
        functools.partial(body, mesh.shape["lat"], mesh.shape["lon"]),
        mesh=mesh,
        in_specs=placed,
        out_specs=(P(None, "lat", "lon"), P()),
        check_vma=False,
    )
```

```python
import functools

import jax
import jax.numpy as jnp
from jax import lax
from jax.experimental import pallas as pl
from jax.experimental.pallas import tpu as pltpu
from jax.sharding import PartitionSpec as P

MESH = pl.DeviceIdType.MESH
HIGHEST = lax.Precision.HIGHEST
misfit_scale = 8.0
DEEP = 8
REACH = 4


def spread(rows):
    count, lanes = rows.shape
    return jnp.broadcast_to(rows[:, None, :], (count, 8, lanes)).reshape(count * 8, lanes)


def kernel(
    dims, prior3, prior2, hab2, kappa, mask, profiles, ids, out2, logev,
    pr, hb, hf, ext, one, lik, ak, aux_lo, aux_hi, bulk_lo, bulk_hi, kb, khb,
    px, px_left, px_right, he, ce, h1, mom, acc, tot1, tot2,
    loc_sem, mom_s, mom_r, px_s, px_r, aux_s, aux_r, bulk_s, bulk_r, cor_s, cor_r,
    t1_s, t1_r, t2_s, t2_r,
):
    n_lat, n_lon, tags, levels, rows, lanes = dims
    groups = tags // 8
    erows = rows + 2 * DEEP
    hrows = rows + 2 * REACH
    half = tags // 2
    lat, lon = lax.axis_index("lat"), lax.axis_index("lon")
    has_lo, has_hi = lat > 0, lat < n_lat - 1
    left, right = lax.rem(lon + n_lon - 1, n_lon), lax.rem(lon + 1, n_lon)

    own_prior = pltpu.make_async_copy(prior2, pr, loc_sem.at[0])
    own_hab = pltpu.make_async_copy(hab2, hb, loc_sem.at[1])
    own_prior.start()
    own_hab.start()

    barrier = pltpu.get_barrier_semaphore()
    for k in range(1, n_lon):
        pl.semaphore_signal(
            barrier, inc=1, device_id={"lon": lax.rem(lon + k, n_lon)}, device_id_type=MESH
        )
    for k in range(1, n_lat):
        pl.semaphore_signal(
            barrier, inc=1, device_id={"lat": lax.rem(lat + k, n_lat)}, device_id_type=MESH
        )

    def remote(src, dst, send, recv, where):
        return pltpu.make_async_remote_copy(
            src_ref=src, dst_ref=dst, send_sem=send, recv_sem=recv, device_id=where,
            device_id_type=MESH,
        )

    lane = lax.broadcasted_iota(jnp.int32, (8, lanes), 1)
    ocean = mask[...].astype(jnp.float32)
    ko = kappa[...] * ocean
    ak[0] = ocean
    ak[1] = ko
    prof = profiles[...]
    local = prof.shape[0]
    squares = jnp.sum(prof * prof, 1, keepdims=True)
    table = jnp.concatenate(
        [
            prof,
            squares,
            jnp.ones((local, 1), jnp.float32),
            jnp.zeros((local, 128 - levels - 2), jnp.float32),
        ],
        axis=1,
    )
    onehot = (
        lax.broadcasted_iota(jnp.int32, (tags, local), 0) == ids[...]
    ).astype(jnp.float32)
    sums = jnp.dot(onehot, table, precision=HIGHEST, preferred_element_type=jnp.float32)
    mom[lon] = sums[:half] + pltpu.roll(sums[half:], 64, 1)
    folded = pltpu.roll(ko, DEEP, 1)
    folded = jnp.where(lax.broadcasted_iota(jnp.int32, (rows, lanes), 1) < 16, folded, 0.0)
    for step in (16, 32, 64):
        folded = folded + pltpu.roll(folded, step, 1)
    px[pl.ds(rows * 8, rows), :] = folded

    own_prior.wait()

    def pack(a, carry):
        wet = jnp.broadcast_to(ak[0, pl.ds(a, 1), :], (8, lanes))
        packed = jnp.zeros((8, lanes), jnp.float32)
        for g in range(groups):
            value = pr[pl.ds(g * 8 * rows + a, 8, stride=rows), :] * wet
            ext[pl.ds(pl.multiple_of((g * erows + DEEP + a) * 8, 8), 8), :] = value
            turned = pltpu.roll(value, (DEEP + 16 * g) % lanes, 1)
            packed = jnp.where((lane >= 16 * g) & (lane < 16 * g + 16), turned, packed)
        px[pl.ds(pl.multiple_of(a * 8, 8), 8), :] = packed
        return carry

    lax.fori_loop(0, rows, pack, 0, unroll=2)

    pl.semaphore_wait(barrier, n_lon - 1 + n_lat - 1)

    to_right = remote(px, px_left, px_s.at[0], px_r.at[0], {"lon": right})
    to_left = remote(px, px_right, px_s.at[1], px_r.at[1], {"lon": left})
    to_right.start()
    to_left.start()

    moment_copies = []
    for k in range(1, n_lon):
        copy = remote(
            mom.at[lon], mom.at[lon], mom_s.at[k - 1], mom_r.at[k - 1],
            {"lon": lax.rem(lon + k, n_lon)},
        )
        copy.start()
        moment_copies.append(copy)

    to_hi_aux = remote(
        ak.at[:, rows - DEEP : rows, :], aux_lo, aux_s.at[0], aux_r.at[0], {"lat": lat + 1}
    )
    to_lo_aux = remote(ak.at[:, 0:DEEP, :], aux_hi, aux_s.at[1], aux_r.at[1], {"lat": lat - 1})

    def to_hi(g):
        return remote(
            prior3.at[pl.ds(g * 8, 8), rows - DEEP : rows, :],
            bulk_lo.at[pl.ds(g * 8, 8)],
            bulk_s.at[0, g],
            bulk_r.at[0, g],
            {"lat": lat + 1},
        )

    def to_lo(g):
        return remote(
            prior3.at[pl.ds(g * 8, 8), 0:DEEP, :],
            bulk_hi.at[pl.ds(g * 8, 8)],
            bulk_s.at[1, g],
            bulk_r.at[1, g],
            {"lat": lat - 1},
        )

    early = groups // 2

    @pl.when(has_hi)
    def _():
        to_hi_aux.start()
        for g in range(early):
            to_hi(g).start()

    @pl.when(has_lo)
    def _():
        to_lo_aux.start()
        for g in range(early):
            to_lo(g).start()

    @pl.when(jnp.logical_not(has_lo))
    def _():
        bulk_lo[...] = jnp.zeros_like(bulk_lo)
        aux_lo[...] = jnp.zeros_like(aux_lo)
        he[0 : REACH * 8, :] = jnp.zeros((REACH * 8, lanes), jnp.float32)

    @pl.when(jnp.logical_not(has_hi))
    def _():
        bulk_hi[...] = jnp.zeros_like(bulk_hi)
        aux_hi[...] = jnp.zeros_like(aux_hi)
        he[(REACH + rows) * 8 : hrows * 8, :] = jnp.zeros((REACH * 8, lanes), jnp.float32)

    kb[REACH * 8 : (REACH + rows) * 8, :] = spread(ak[1])
    def lon_sum(low, high):
        total = pltpu.roll(low, REACH, 1) + pltpu.roll(high, lanes - REACH, 1)
        for d in range(1, REACH):
            total = total + (5.0 - d) * (pltpu.roll(low, d, 1) + pltpu.roll(high, lanes - d, 1))
        return total

    def lat_sum(ref, at):
        total = ref[pl.ds(at - 8 * REACH, 64), :] + ref[pl.ds(at + 8 * REACH, 64), :]
        for d in range(1, REACH):
            total = total + (5.0 - d) * (
                ref[pl.ds(at - 8 * d, 64), :] + ref[pl.ds(at + 8 * d, 64), :]
            )
        return total

    weights = [
        (
            jnp.concatenate([jnp.where(lane >= d, 5.0 - d, 0.0)] * 8, axis=0),
            jnp.concatenate([jnp.where(lane < lanes - d, 5.0 - d, 0.0)] * 8, axis=0),
        )
        for d in range(1, REACH + 1)
    ]
    at_edge = jnp.concatenate([(lane < REACH) | (lane >= lanes - REACH)] * 8, axis=0)
    def place(sides, shift):
        return jnp.where(at_edge, pltpu.roll(sides, shift, 1), 0.0)

    def sweep(center, coeff, ref, at, edge):
        along = lat_sum(ref, at)
        for d in range(1, REACH + 1):
            up, down = weights[d - 1]
            along = along + up * pltpu.roll(center, d, 1) + down * pltpu.roll(center, lanes - d, 1)
        along = 0.1 * along - 4.0 * center
        if edge is not None:
            along = along + edge
        return center + coeff * along

    def inside(g, carry):
        base = g * erows * 8
        for b in range(1, rows // 8):
            at = pl.multiple_of(base + (REACH + 8 * b) * 8, 8)
            one[pl.ds(pl.multiple_of(g * hrows * 8 + b * 64, 8), 64), :] = sweep(
                ext[pl.ds(at, 64), :], kb[b * 64 : b * 64 + 64, :], ext, at, None
            )
        return carry

    lax.fori_loop(0, groups, inside, 0)

    to_right.wait()
    to_left.wait()
    low_side = lax.rem(lax.broadcasted_iota(jnp.int32, (64, lanes), 1), 16) < 8
    for b in range(rows // 8):
        he[(REACH + 8 * b) * 8 : (REACH + 8 * b + 8) * 8, :] = jnp.where(
            low_side, px_left[b * 64 : b * 64 + 64, :], px_right[b * 64 : b * 64 + 64, :]
        )
    low_rows = lax.rem(lax.broadcasted_iota(jnp.int32, (rows, lanes), 1), 16) < 8
    ko_side = jnp.where(
        low_rows, px_left[rows * 8 : rows * 9, :], px_right[rows * 8 : rows * 9, :]
    )
    khb[...] = spread(ko_side)

    cor_hi = remote(
        he.at[rows * 8 : (rows + REACH) * 8, :], he.at[0 : REACH * 8, :],
        cor_s.at[0], cor_r.at[0], {"lat": lat + 1},
    )
    cor_lo = remote(
        he.at[REACH * 8 : 2 * REACH * 8, :], he.at[(REACH + rows) * 8 : hrows * 8, :],
        cor_s.at[1], cor_r.at[1], {"lat": lat - 1},
    )

    @pl.when(has_hi)
    def _():
        cor_hi.start()
        for g in range(early, groups):
            to_hi(g).start()

    @pl.when(has_lo)
    def _():
        cor_lo.start()
        for g in range(early, groups):
            to_lo(g).start()

    own_hab.wait()
    hf[...] = hb[...].astype(jnp.float32)
    for copy in moment_copies:
        copy.wait()
    total_moments = mom[0]
    for k in range(1, n_lon):
        total_moments = total_moments + mom[k]
    moments = jnp.concatenate([total_moments, pltpu.roll(total_moments, 64, 1)], axis=0)
    tag_lane = lax.broadcasted_iota(jnp.int32, (tags, lanes), 1)
    second = jnp.broadcast_to(moments[:, levels : levels + 1], (tags, lanes))
    count = jnp.broadcast_to(moments[:, levels + 1 : levels + 2], (tags, lanes))
    first = jnp.where(tag_lane < levels, moments, 0.0)
    top = first.astype(jnp.bfloat16).astype(jnp.float32)
    rest = first - top
    middle = rest.astype(jnp.bfloat16).astype(jnp.float32)
    bottom = (rest - middle).astype(jnp.bfloat16).astype(jnp.float32)
    split = (top + pltpu.roll(middle, levels, 1) + pltpu.roll(bottom, 2 * levels, 1)).astype(
        jnp.bfloat16
    )
    pad = jnp.zeros((lanes - 3 * levels, lanes), jnp.bfloat16)

    def likelihood(a, carry):
        field = hf[pl.ds(a, levels, stride=rows), :]
        square = jnp.sum(field * field, 0, keepdims=True)
        narrow = field.astype(jnp.bfloat16)
        crossed = jnp.dot(
            split,
            jnp.concatenate([narrow, narrow, narrow, pad], axis=0),
            preferred_element_type=jnp.float32,
        )
        misfit = second - 2.0 * crossed + count * square
        value = jnp.exp(misfit * (-1.0 / (misfit_scale * levels)))
        for g in range(groups):
            lik[pl.ds(pl.multiple_of((g * rows + a) * 8, 8), 8), :] = value[g * 8 : g * 8 + 8]
        return carry

    lax.fori_loop(0, rows, likelihood, 0, unroll=2)

    @pl.when(has_lo)
    def _():
        to_hi_aux.wait_recv()
        cor_hi.wait_recv()

    @pl.when(has_hi)
    def _():
        to_lo_aux.wait_recv()
        cor_lo.wait_recv()

    kb[0 : REACH * 8, :] = spread(aux_lo[1])[REACH * 8 :]
    kb[(REACH + rows) * 8 :, :] = spread(aux_hi[1])[: REACH * 8]

    def across(field):
        from_low = jnp.where(low_side, field, 0.0)
        from_high = jnp.where(low_side, 0.0, field)
        low, high = pltpu.roll(from_low, REACH, 1), pltpu.roll(from_high, lanes - REACH, 1)
        for d in range(1, REACH):
            low = low + (5.0 - d) * pltpu.roll(from_low, d, 1)
            high = high + (5.0 - d) * pltpu.roll(from_high, lanes - d, 1)
        return jnp.where(low_side, high, low)

    for b in range(hrows // 8):
        ce[b * 64 : b * 64 + 64, :] = 0.1 * across(he[b * 64 : b * 64 + 64, :])

    for b in range(rows // 8):
        at = (REACH + 8 * b) * 8
        side = he[at : at + 64, :]
        inner = px[b * 64 : b * 64 + 64, :]
        z_left = jnp.where(low_side, side, inner)
        z_right = jnp.where(low_side, inner, side)
        along = jnp.where(low_side, lon_sum(z_left, z_left), lon_sum(z_right, z_right))
        h1[b * 64 : b * 64 + 64, :] = 0.1 * across(
            side
            + khb[b * 64 : b * 64 + 64, :] * (0.1 * (along + lat_sum(he, at)) - 4.0 * side)
        )

    low_flat = bulk_lo.reshape(tags * DEEP, lanes)
    high_flat = bulk_hi.reshape(tags * DEEP, lanes)
    acc[...] = jnp.zeros_like(acc)

    def group(g, carry):
        @pl.when(has_lo)
        def _():
            to_hi(g).wait_recv()

        @pl.when(has_hi)
        def _():
            to_lo(g).wait_recv()

        base = g * erows * 8
        for a in range(DEEP):
            ext[pl.ds(pl.multiple_of(base + a * 8, 8), 8), :] = low_flat[
                pl.ds(g * 64 + a, 8, stride=DEEP), :
            ] * jnp.broadcast_to(aux_lo[0, a : a + 1, :], (8, lanes))
            ext[pl.ds(pl.multiple_of(base + (DEEP + rows + a) * 8, 8), 8), :] = high_flat[
                pl.ds(g * 64 + a, 8, stride=DEEP), :
            ] * jnp.broadcast_to(aux_hi[0, a : a + 1, :], (8, lanes))
        shift = lax.rem(lanes - DEEP - 16 * g + lanes, lanes)
        first_row = g * hrows * 8
        for b in range(hrows // 8):
            at = pl.multiple_of(base + (REACH + 8 * b) * 8, 8)
            there = pl.ds(pl.multiple_of(first_row + b * 64, 8), 64)
            coeff = kb[b * 64 : b * 64 + 64, :]
            edge = place(ce[b * 64 : b * 64 + 64, :], shift)
            if 1 <= b < rows // 8:
                one[there, :] = one[there, :] + coeff * edge
            else:
                one[there, :] = sweep(ext[pl.ds(at, 64), :], coeff, ext, at, edge)
        partial = jnp.zeros((8, lanes), jnp.float32)
        for b in range(rows // 8):
            start = (REACH + 8 * b) * 8
            at = pl.multiple_of(first_row + start, 8)
            here = pl.ds(pl.multiple_of(g * rows * 8 + b * 64, 8), 64)
            updated = (
                sweep(
                    one[pl.ds(at, 64), :],
                    kb[start : start + 64, :],
                    one,
                    at,
                    place(h1[b * 64 : b * 64 + 64, :], shift),
                )
                * lik[here, :]
            )
            lik[here, :] = updated
            partial = partial + jnp.sum(updated.reshape(8, 8, lanes), 0)
        acc[pl.ds(pl.multiple_of(g * 8, 8), 8), :] = partial
        return carry

    lax.fori_loop(0, groups, group, 0)

    row = lax.dot_general(
        jnp.ones((8, lanes), jnp.float32), acc[...], (((1,), (1,)), ((), ())),
        precision=HIGHEST, preferred_element_type=jnp.float32,
    )
    tot1[lon] = row[0:1]
    copies = []
    for k in range(1, n_lon):
        copy = remote(
            tot1.at[lon], tot1.at[lon], t1_s.at[k - 1], t1_r.at[k - 1],
            {"lon": lax.rem(lon + k, n_lon)},
        )
        copy.start()
        copies.append(copy)
    for copy in copies:
        copy.wait()
    total = tot1[0]
    for k in range(1, n_lon):
        total = total + tot1[k]
    tot2[lat] = total
    copies = []
    for k in range(1, n_lat):
        copy = remote(
            tot2.at[lat], tot2.at[lat], t2_s.at[k - 1], t2_r.at[k - 1],
            {"lat": lax.rem(lat + k, n_lat)},
        )
        copy.start()
        copies.append(copy)
    for copy in copies:
        copy.wait()
    total = tot2[0]
    for k in range(1, n_lat):
        total = total + tot2[k]
    cells = float(n_lat * n_lon * rows * lanes)
    logev[...] = jnp.log(total[:, :tags] / cells)
    first_row = lax.broadcasted_iota(jnp.int32, (8, lanes), 0) == 0
    column = lax.dot_general(
        jnp.where(first_row, jnp.broadcast_to(total, (8, lanes)), 0.0),
        jnp.ones((8, lanes), jnp.float32),
        (((0,), (0,)), ((), ())),
        precision=HIGHEST, preferred_element_type=jnp.float32,
    )
    acc[...] = cells / column

    def finish(a, carry):
        for g in range(groups):
            out2[pl.ds(g * 8 * rows + a, 8, stride=rows), :] = (
                lik[pl.ds(pl.multiple_of((g * rows + a) * 8, 8), 8), :]
                * acc[g * 8 : g * 8 + 8, :]
            )
        return carry

    lax.fori_loop(0, rows, finish, 0, unroll=2)

    @pl.when(has_hi)
    def _():
        to_hi_aux.wait_send()
        cor_hi.wait_send()
        for g in range(groups):
            to_hi(g).wait_send()

    @pl.when(has_lo)
    def _():
        to_lo_aux.wait_send()
        cor_lo.wait_send()
        for g in range(groups):
            to_lo(g).wait_send()


def body(n_lat, n_lon, prior, habitat, kappa, ocean_mask, profiles, tag_ids):
    tags, rows, lanes = prior.shape
    levels = habitat.shape[0]
    groups = tags // 8
    erows, hrows = rows + 2 * DEEP, rows + 2 * REACH
    f32 = jnp.float32
    flat = (tags * rows, lanes)
    vmem = pl.BlockSpec(memory_space=pltpu.VMEM)
    hbm = pl.BlockSpec(memory_space=pl.ANY)
    dma = pltpu.SemaphoreType.DMA
    posterior, logev = pl.pallas_call(
        functools.partial(kernel, (n_lat, n_lon, tags, levels, rows, lanes)),
        name="filter_step",
        out_shape=(jax.ShapeDtypeStruct(flat, f32), jax.ShapeDtypeStruct((1, tags), f32)),
        in_specs=[hbm, hbm, hbm, vmem, vmem, vmem, vmem],
        out_specs=(vmem, vmem),
        scratch_shapes=[
            pltpu.VMEM(flat, f32),
            pltpu.VMEM((levels * rows, lanes), habitat.dtype),
            pltpu.VMEM((levels * rows, lanes), f32),
            pltpu.VMEM((groups * erows * 8, lanes), f32),
            pltpu.VMEM((groups * hrows * 8, lanes), f32),
            pltpu.VMEM((groups * rows * 8, lanes), f32),
            pltpu.VMEM((2, rows, lanes), f32),
            pltpu.VMEM((2, DEEP, lanes), f32),
            pltpu.VMEM((2, DEEP, lanes), f32),
            pltpu.VMEM((tags, DEEP, lanes), f32),
            pltpu.VMEM((tags, DEEP, lanes), f32),
            pltpu.VMEM((hrows * 8, lanes), f32),
            pltpu.VMEM((rows * 8, lanes), f32),
            pltpu.VMEM((rows * 9, lanes), f32),
            pltpu.VMEM((rows * 9, lanes), f32),
            pltpu.VMEM((rows * 9, lanes), f32),
            pltpu.VMEM((hrows * 8, lanes), f32),
            pltpu.VMEM((hrows * 8, lanes), f32),
            pltpu.VMEM((rows * 8, lanes), f32),
            pltpu.VMEM((n_lon, tags // 2, lanes), f32),
            pltpu.VMEM((lanes, lanes), f32),
            pltpu.VMEM((n_lon, 1, lanes), f32),
            pltpu.VMEM((n_lat, 1, lanes), f32),
            dma((2,)),
            dma((n_lon - 1,)),
            dma((n_lon - 1,)),
            dma((2,)),
            dma((2,)),
            dma((2,)),
            dma((2,)),
            dma((2, groups)),
            dma((2, groups)),
            dma((2,)),
            dma((2,)),
            dma((n_lon - 1,)),
            dma((n_lon - 1,)),
            dma((n_lat - 1,)),
            dma((n_lat - 1,)),
        ],
        compiler_params=pltpu.CompilerParams(collective_id=0, has_side_effects=True),
    )(
        prior,
        prior.reshape(flat),
        habitat.reshape(levels * rows, lanes),
        kappa,
        ocean_mask,
        profiles,
        tag_ids[None, :],
    )
    return posterior.reshape(prior.shape), logev[0]


def solution(mesh):
    placed = (
        P(None, "lat", "lon"),
        P(None, "lat", "lon"),
        P("lat", "lon"),
        P("lat", "lon"),
        P("lon", None),
        P("lon"),
    )
    return jax.shard_map(
        functools.partial(body, mesh.shape["lat"], mesh.shape["lon"]),
        mesh=mesh,
        in_specs=placed,
        out_specs=(P(None, "lat", "lon"), P()),
        check_vma=False,
    )
```
